32 devices in a mesh: seq: 16 (over z, x, core), head: 2 (over y).
Axes of the slice: x: 2, y: 2, z: 4, core: 2. Of those that a mesh axis runs over, the one named last changes fastest.
Arguments:
- byte_rows: bfloat16 [16384, 1024], P('seq', 'head'), may hold values from -6 to 6
- pool_weight: bfloat16 [4, 1024, 1024], P(None, 'head'), may hold values from -0.09375 to 0.09375
- norm_gain: float32 [1024], replicated, may hold values from 0.1 to 1.9
- qkv_weight: bfloat16 [1024, 8, 3, 128], P(None, 'head')
- span_order: int32 [16], replicated, may hold values from 0 to 15, as said below
- query_start: int32 [1], replicated, may hold values from 2560 to 3072
Outputs:
- shortened: bfloat16 [4096, 1024], P('seq', 'head')
- context: bfloat16 [1024, 1024], P('seq', 'head')
- row_highest: float32 [8, 1024], P('head', 'seq')
The draws below stay inside these ranges and needn't reach their ends.
Inputs may be any that keep to these rules, and one draw needn't show every extreme that they name: `span_order`: entry i is (i + r) mod 16 for one r of each draw.
All inputs are finite; a program needn't handle non-finite values.
Results may differ from the reference program's by a relative error of at most 0.015.
Values may be sent and summed in bfloat16 or wider, within the bound.
A program may use at most 64 MiB of HBM per device.

```python
import jax
import jax.numpy as jnp
from jax import lax

D = 1024
HEADS = 8
HEAD_DIM = 128
SF = 4
SPAN = 128
PAIRS = 16
SHORT = 4096
BYTES = 16384
QUERIES = 1024


def draw_span_order(key, part):
    rotation = jax.random.randint(key, (), 0, PAIRS)
    return ((jnp.arange(PAIRS, dtype=jnp.int32) + rotation) % PAIRS).astype(jnp.int32)


def draw_qkv_weight(key, part):
    key_query, key_key, key_value = jax.random.split(jax.random.fold_in(key, 11), 3)
    spread = D ** (-0.5)
    query_part = jax.random.normal(key_query, (D, HEADS, 1, HEAD_DIM), jnp.float32) * spread
    value_part = jax.random.normal(key_value, (D, HEADS, 1, HEAD_DIM), jnp.float32) * spread
    noise_part = jax.random.normal(key_key, (D, HEADS, 1, HEAD_DIM), jnp.float32) * spread
    key_part = noise_part
    return jnp.concatenate([query_part, key_part, value_part], axis=2).astype(jnp.bfloat16)


def levels(key, extent, pieces, least, top_value):
    factor_of, own = 1.0, jax.random.fold_in(key, 6)
    for axis_at, shards_of in pieces:
        steps = jnp.exp(jax.random.uniform(jax.random.fold_in(own, axis_at), (shards_of,), jnp.float32, least / len(pieces), top_value / len(pieces)))
        factor_of = factor_of * jnp.repeat(steps, extent[axis_at] // shards_of).reshape([-1 if axis == axis_at else 1 for axis in range(len(extent))])
    return factor_of


def bell_draw(key, shape, scale, most, cuts=(), kind=jnp.bfloat16):
    factor_of = levels(key, shape, cuts, -0.22, 0.18) if cuts else 1.0
    drawn = jax.random.normal(key, shape, jnp.float32) * scale * factor_of
    return jnp.minimum(jnp.maximum(drawn, -most), most).astype(kind)


def setup_inputs(seed: int = 0) -> dict:
    streams_of = jax.random.split(jax.random.key(seed), 7)
    return {
        "byte_rows": bell_draw(streams_of[0], (BYTES, D), 1.0, 6.0, ((0, 16), (1, 2))),
        "pool_weight": bell_draw(streams_of[1], (SF, D, D), (SF * D) ** -0.5, 0.09375, ((1, 2),)),
        "norm_gain": jnp.clip(1.0 + 0.18 * jax.random.normal(streams_of[2], (D,), jnp.float32), 0.1, 1.9),
        "qkv_weight": draw_qkv_weight(jax.random.fold_in(streams_of[6], 71), 0),
        "span_order": draw_span_order(jax.random.fold_in(streams_of[6], 71), 0),
        "query_start": jax.random.randint(streams_of[5], (1,), SHORT - QUERIES - SHORT // 8, SHORT - QUERIES + 1).astype(jnp.int32),
    }


norm_epsilon = 1e-06
masked_score = -1e+30

def reference(byte_rows, pool_weight, norm_gain, qkv_weight, span_order, query_start):
    pair_count = PAIRS
    span_bytes = SF * SPAN
    pair_slots = jnp.arange(pair_count, dtype=jnp.int32)
    holder = jnp.zeros((pair_count,), jnp.int32).at[span_order].set(pair_slots)
    stored = byte_rows.reshape(pair_count, 2, span_bytes, D)
    ordered = jnp.concatenate([stored[holder, 0], stored[holder[::-1], 1]], axis=0).reshape(BYTES, D)
    shifted = jnp.concatenate([jnp.zeros((SF - 1, D), byte_rows.dtype), ordered[:BYTES - (SF - 1)]], axis=0)
    grouped = shifted.reshape(SHORT, SF * D)
    pooled = jnp.dot(grouped, pool_weight.reshape(SF * D, D), preferred_element_type=jnp.float32).astype(jnp.bfloat16)
    widened = pooled.astype(jnp.float32)
    squares = lax.optimization_barrier(jnp.sum(widened * widened, axis=1, keepdims=True)) / D
    normed = (widened * lax.rsqrt(squares + norm_epsilon) * norm_gain).astype(jnp.bfloat16)
    projected = jnp.dot(normed, qkv_weight.reshape(D, HEADS * 3 * HEAD_DIM), preferred_element_type=jnp.float32)
    projected = projected.astype(jnp.bfloat16).reshape(SHORT, HEADS, 3, HEAD_DIM)
    window_start = query_start[0].astype(jnp.int32)
    queries = lax.dynamic_slice_in_dim(projected[:, :, 0], window_start, QUERIES, 0).astype(jnp.float32)
    key_rows = projected[:, :, 1].astype(jnp.float32)
    value_rows = projected[:, :, 2].astype(jnp.float32)
    key_pos = jnp.arange(SHORT, dtype=jnp.int32)
    score_scale = HEAD_DIM ** (-0.5)
    step_rows = min(256, QUERIES)

    def attend(block_index):
        query_block = lax.dynamic_slice_in_dim(queries, (block_index * step_rows).astype(jnp.int32), step_rows, 0)
        query_pos = window_start + block_index * step_rows + jnp.arange(step_rows, dtype=jnp.int32)
        scores = jnp.einsum('qhd,khd->hqk', query_block, key_rows) * score_scale
        scores = jnp.where(key_pos[None, None, :] <= query_pos[None, :, None], scores, masked_score)
        highest = lax.optimization_barrier(jnp.max(scores, axis=2, keepdims=True))
        rounded = lax.optimization_barrier(jnp.exp(scores - highest).astype(jnp.bfloat16))
        weights = rounded.astype(jnp.float32)
        totals = lax.optimization_barrier(jnp.sum(weights, axis=2))
        summed = jnp.einsum('hqk,khd->qhd', weights, value_rows)
        return ((summed / totals.T[:, :, None]).astype(jnp.bfloat16), highest[:, :, 0])
    context, maxima = lax.map(attend, jnp.arange(QUERIES // step_rows, dtype=jnp.int32))
    context = context.reshape(QUERIES, D)
    row_highest = jnp.transpose(maxima, (1, 0, 2)).reshape(HEADS, QUERIES) * HEAD_DIM ** 0.5
    placed_ids = jnp.stack([span_order, 2 * pair_count - 1 - span_order], axis=1).reshape(2 * pair_count).astype(jnp.int32)
    shortened = pooled.reshape(2 * pair_count, SPAN, D)[placed_ids].reshape(SHORT, D)
    return (shortened, context, row_highest)
```

```python
import jax
import jax.numpy as jnp
from jax import lax
from jax.sharding import PartitionSpec as P

SF = 4
QROWS_DEV = 64


norm_epsilon = 1e-06
masked_score = -1e30


def ring(count, step):
    return [(i, (i + step) % count) for i in range(count)]


def body(byte_rows, pool_weight, norm_gain, qkv_weight, span_order, query_start):
    local_rows, features = byte_rows.shape
    half_rows = local_rows // 2
    short_rows = local_rows // SF
    span_rows = short_rows // 2
    model_width = qkv_weight.shape[0]
    heads_here = qkv_weight.shape[1]
    head_width = qkv_weight.shape[3]
    width_here = heads_here * head_width
    pair_count = lax.axis_size("seq")
    head_count = lax.axis_size("head")
    seq_index = lax.axis_index("seq")
    head_index = lax.axis_index("head")
    pair_slots = jnp.arange(pair_count, dtype=jnp.int32)
    my_pair = jnp.sum(jnp.where(pair_slots == seq_index, span_order, 0))
    shift_rows = SF - 1
    first_tail = byte_rows[half_rows - shift_rows : half_rows]
    last_tail = byte_rows[local_rows - shift_rows :]
    from_before = lax.ppermute(first_tail, "seq", ring(pair_count, 1))
    from_after = lax.ppermute(last_tail, "seq", ring(pair_count, -1))
    first_prev = jnp.where(my_pair == 0, jnp.zeros_like(from_before), from_before)
    second_prev = jnp.where(my_pair == pair_count - 1, first_tail, from_after)
    grouped = jnp.concatenate(
        [
            first_prev,
            byte_rows[: half_rows - shift_rows],
            second_prev,
            byte_rows[half_rows : local_rows - shift_rows],
        ],
        axis=0,
    )
    grouped = grouped.reshape(short_rows, SF * features)
    partial = jnp.dot(
        grouped, pool_weight.reshape(SF * features, model_width), preferred_element_type=jnp.float32
    )
    sent = partial.astype(jnp.bfloat16)
    total = partial
    for step in range(1, head_count):
        total = total + lax.ppermute(sent, "head", ring(head_count, step)).astype(jnp.float32)
    pooled = total.astype(jnp.bfloat16)
    shortened = lax.dynamic_slice_in_dim(pooled, head_index * features, features, 1)
    widened = pooled.astype(jnp.float32)
    squares = jnp.sum(widened * widened, axis=1, keepdims=True) / model_width
    normed = (widened * lax.rsqrt(squares + norm_epsilon) * norm_gain).astype(jnp.bfloat16)
    projected = jnp.einsum(
        "rm,mhtd->thrd", normed, qkv_weight, preferred_element_type=jnp.float32
    ).astype(jnp.bfloat16)
    keys, values = projected[1], projected[2]
    half_short = pair_count * span_rows
    query_total = QROWS_DEV * pair_count
    window_start = query_start[0]
    late = lax.all_gather(projected[0][:, span_rows:], "seq", axis=0, tiled=False)
    late = jnp.concatenate([late[::-1], late[::-1]], axis=0)
    late = late.transpose(1, 0, 2, 3).reshape(heads_here, 2 * half_short, head_width)
    at_row = span_order[0] * span_rows + window_start - half_short
    queries = lax.dynamic_slice_in_dim(late, at_row, query_total, 1)
    score_scale = head_width ** (-0.5)
    local = jnp.arange(short_rows, dtype=jnp.int32)
    span_id = jnp.where(local < span_rows, my_pair, 2 * pair_count - 1 - my_pair)
    key_pos = span_id * span_rows + local % span_rows
    query_pos = window_start + jnp.arange(query_total, dtype=jnp.int32)
    scores = (
        jnp.einsum("hqd,hkd->hqk", queries, keys, preferred_element_type=jnp.float32) * score_scale
    )
    scores = jnp.where(key_pos[None, None, :] <= query_pos[None, :, None], scores, masked_score)
    highest = jnp.max(scores, axis=2)
    weights = jnp.exp(scores - highest[:, :, None]).astype(jnp.bfloat16)
    totals = jnp.sum(weights, axis=2, dtype=jnp.float32)
    summed = jnp.einsum("hqk,hkd->qhd", weights, values, preferred_element_type=jnp.float32)
    summed = summed.astype(jnp.bfloat16).reshape(query_total, width_here)
    stats = jnp.stack([highest, totals], axis=0).reshape(2, heads_here, pair_count, QROWS_DEV)
    stats = stats.transpose(2, 0, 1, 3)
    summed = lax.all_to_all(summed, "seq", split_axis=0, concat_axis=0, tiled=True)
    stats = lax.all_to_all(stats, "seq", split_axis=0, concat_axis=0, tiled=True)
    summed = summed.reshape(pair_count, QROWS_DEV, heads_here, head_width).astype(jnp.float32)
    highs, tots = stats[:, 0], stats[:, 1]
    top = jnp.max(highs, axis=0)
    factor = jnp.exp(highs - top[None])
    denominator = jnp.sum(factor * tots, axis=0)
    numerator = jnp.sum(summed * factor.transpose(0, 2, 1)[..., None], axis=0)
    context = numerator / denominator.T[:, :, None]
    row_highest = top * head_width**0.5
    return (
        shortened,
        context.reshape(QROWS_DEV, width_here).astype(jnp.bfloat16),
        row_highest,
    )


def solution(mesh):
    placed = (P("seq", "head"), P(None, "head", None), P(), P(None, "head", None, None), P(), P())
    return jax.shard_map(
        body,
        mesh=mesh,
        in_specs=placed,
        out_specs=(P("seq", "head"), P("seq", "head"), P("head", "seq")),
        check_vma=False,
    )
```

```python
import functools

import jax
import jax.numpy as jnp
from jax import lax
from jax.experimental import pallas as pl
from jax.experimental.pallas import tpu as pltpu
from jax.sharding import PartitionSpec as P

SF = 4
QROWS_DEV = 64


norm_epsilon = 1e-06
masked_score = -1e30


def ring(count, step):
    return [(i, (i + step) % count) for i in range(count)]


LANES = 128
STAT_STEP = 16


def pack_stats(highest, totals):
    high_top = highest.astype(jnp.bfloat16).astype(jnp.float32)
    rest = highest - high_top
    high_mid = rest.astype(jnp.bfloat16).astype(jnp.float32)
    high_low = rest - high_mid
    total_top = totals.astype(jnp.bfloat16).astype(jnp.float32)
    total_low = totals - total_top
    packed = high_top
    for place, piece in enumerate((high_mid, high_low, total_top, total_low)):
        packed = packed + pltpu.roll(piece, STAT_STEP * (place + 1), 1)
    return packed


def unpack_stats(packed):
    def piece(place):
        return pltpu.roll(packed, LANES - STAT_STEP * place, 1)

    return packed + piece(1) + piece(2), piece(3) + piece(4)


def attend_kernel(
    count, heads, width, numbers, projected, context, top_out,
    gathered, parts, arrived, gather_send, gather_recv, part_send, part_recv,
):
    me = lax.axis_index("seq")
    core = lax.rem(me, 2)
    middle = lax.rem(me // 2, 2)
    outer = me // 4
    outers = count // 4
    rows = projected.shape[0]
    span = rows // 2
    total_width = heads * width

    def at(outer_at, middle_at, core_at):
        return (lax.rem(outer_at, outers) * 2 + middle_at) * 2 + core_at

    barrier = pltpu.get_barrier_semaphore()

    def greet(step, carry):
        pl.semaphore_signal(
            barrier, inc=1, device_id={"seq": lax.rem(me + step, count)},
            device_id_type=pl.DeviceIdType.MESH,
        )
        return carry

    lax.fori_loop(1, count, greet, 0)
    for head in range(heads):
        gathered[me, :, head * width : (head + 1) * width] = projected[
            span:, head * 3 * width : (head * 3 + 1) * width
        ]
    pl.semaphore_wait(barrier, count - 1)

    pushes = []

    def push(slot, target):
        copy = pltpu.make_async_remote_copy(
            src_ref=gathered.at[slot], dst_ref=gathered.at[slot],
            send_sem=gather_send.at[len(pushes)], recv_sem=gather_recv.at[slot],
            device_id={"seq": target}, device_id_type=pl.DeviceIdType.MESH,
        )
        copy.start()
        pushes.append(copy)

    def landed(slot):
        pltpu.make_async_remote_copy(
            src_ref=gathered.at[slot], dst_ref=gathered.at[slot],
            send_sem=gather_send.at[0], recv_sem=gather_recv.at[slot],
            device_id={"seq": at(outer, middle, 1 - core)},
            device_id_type=pl.DeviceIdType.MESH,
        ).wait_recv()

    across = at(outer, 1 - middle, core)
    sibling = at(outer, middle, 1 - core)
    for step in range(1, outers):
        push(me, at(outer + step, middle, core))
    push(me, across)
    push(me, sibling)
    for step in range(1, outers):
        slot = at(outer + step, middle, core)
        landed(slot)
        push(slot, across)
        push(slot, sibling)
    for step in range(outers):
        slot = at(outer + step, 1 - middle, core)
        landed(slot)
        push(slot, sibling)
    for step in range(outers):
        landed(at(outer + step, middle, 1 - core))
        landed(at(outer + step, 1 - middle, 1 - core))

    blocks = count // 2
    offset = numbers[2 * blocks]
    first_base = numbers[2 * blocks + 1]
    second_base = numbers[2 * blocks + 2]
    window_start = numbers[2 * blocks + 3]
    pick_row = lax.broadcasted_iota(jnp.int32, (span, 2 * span), 0)
    pick_col = lax.broadcasted_iota(jnp.int32, (span, 2 * span), 1)
    pick = jnp.where(pick_col == pick_row + offset, 1.0, 0.0).astype(jnp.bfloat16)
    key_col = lax.broadcasted_iota(jnp.int32, (span, rows), 1)
    key_pos = jnp.where(key_col < span, first_base + key_col, second_base + key_col - span)
    ahead = key_pos - lax.broadcasted_iota(jnp.int32, (span, rows), 0) - window_start
    lane = lax.broadcasted_iota(jnp.int32, (span, LANES), 1)
    scale = width ** (-0.5)

    def part_copy(target):
        return pltpu.make_async_remote_copy(
            src_ref=parts.at[target], dst_ref=arrived.at[me],
            send_sem=part_send.at[target], recv_sem=part_recv.at[me],
            device_id={"seq": target}, device_id_type=pl.DeviceIdType.MESH,
        )

    def attend(step, carry):
        block = lax.rem(me // 2 + 1 + step, blocks)
        both = jnp.concatenate(
            [gathered[numbers[block]], gathered[numbers[blocks + block]]], axis=0
        )
        queries = jnp.dot(pick, both, preferred_element_type=jnp.float32).astype(jnp.bfloat16)
        allowed = ahead <= block * span
        highs = jnp.zeros((span, LANES), jnp.float32)
        totals = jnp.zeros((span, LANES), jnp.float32)
        for head in range(heads):
            base = head * 3 * width
            keys = projected[:, base + width : base + 2 * width]
            values = projected[:, base + 2 * width : base + 3 * width]
            scores = lax.dot_general(
                queries[:, head * width : (head + 1) * width], keys,
                (((1,), (1,)), ((), ())), preferred_element_type=jnp.float32,
            ) * scale
            scores = jnp.where(allowed, scores, masked_score)
            high = jnp.max(scores, axis=1, keepdims=True)
            weights = jnp.exp(scores - high).astype(jnp.bfloat16)
            total = jnp.sum(weights.astype(jnp.float32), axis=1, keepdims=True)
            summed = jnp.dot(weights, values, preferred_element_type=jnp.float32)
            summed = summed.astype(jnp.bfloat16)
            columns = slice(head * width, (head + 1) * width)
            parts[2 * block, :, columns] = summed[: span // 2]
            parts[2 * block + 1, :, columns] = summed[span // 2 :]
            highs = jnp.where(lane == head, high, highs)
            totals = jnp.where(lane == head, total, totals)
        packed = pack_stats(highs, totals).astype(jnp.bfloat16)
        parts[2 * block, :, total_width:] = packed[: span // 2]
        parts[2 * block + 1, :, total_width:] = packed[span // 2 :]
        for side in range(2):
            target = 2 * block + side

            @pl.when(target != me)
            def _():
                part_copy(target).start()

        return carry

    lax.fori_loop(0, blocks, attend, 0)
    arrived[me] = parts[me]

    def settle(step, carry):
        source = lax.rem(me + step, count)
        pltpu.make_async_remote_copy(
            src_ref=parts.at[source], dst_ref=arrived.at[source],
            send_sem=part_send.at[source], recv_sem=part_recv.at[source],
            device_id={"seq": source}, device_id_type=pl.DeviceIdType.MESH,
        ).wait()
        return carry

    lax.fori_loop(1, count, settle, 0)
    for copy in pushes:
        copy.wait_send()

    def stats_of(source):
        return unpack_stats(arrived[source, :, total_width:].astype(jnp.float32))

    top = lax.fori_loop(
        1, count, lambda source, best: jnp.maximum(best, stats_of(source)[0]), stats_of(0)[0]
    )
    def add(source, carry):
        denominator, pieces = carry
        highs, totals = stats_of(source)
        factor = jnp.exp(highs - top)
        pieces = tuple(
            pieces[head]
            + arrived[source, :, head * width : (head + 1) * width].astype(jnp.float32)
            * factor[:, head : head + 1]
            for head in range(heads)
        )
        return denominator + factor * totals, pieces

    empty = jnp.zeros((span // 2, width), jnp.float32)
    denominator, pieces = lax.fori_loop(
        0, count, add, (jnp.zeros((span // 2, LANES), jnp.float32), (empty,) * heads)
    )
    for head in range(heads):
        context[:, head * width : (head + 1) * width] = (
            pieces[head] / denominator[:, head : head + 1]
        ).astype(jnp.bfloat16)
    top_out[...] = top * width**0.5


def attend_all(numbers, projected, count, heads, width):
    span = projected.shape[0] // 2
    total_width = heads * width
    return pl.pallas_call(
        functools.partial(attend_kernel, count, heads, width),
        out_shape=(
            jax.ShapeDtypeStruct((span // 2, total_width), jnp.bfloat16),
            jax.ShapeDtypeStruct((span // 2, LANES), jnp.float32),
        ),
        in_specs=[
            pl.BlockSpec(memory_space=pltpu.SMEM),
            pl.BlockSpec(memory_space=pltpu.VMEM),
        ],
        out_specs=(
            pl.BlockSpec(memory_space=pltpu.VMEM),
            pl.BlockSpec(memory_space=pltpu.VMEM),
        ),
        scratch_shapes=[
            pltpu.VMEM((count, span, total_width), jnp.bfloat16),
            pltpu.VMEM((count, span // 2, total_width + LANES), jnp.bfloat16),
            pltpu.VMEM((count, span // 2, total_width + LANES), jnp.bfloat16),
            pltpu.SemaphoreType.DMA((count,)),
            pltpu.SemaphoreType.DMA((count,)),
            pltpu.SemaphoreType.DMA((count,)),
            pltpu.SemaphoreType.DMA((count,)),
        ],
        compiler_params=pltpu.CompilerParams(
            collective_id=0, has_side_effects=True, vmem_limit_bytes=40 * 1024 * 1024
        ),
    )(numbers, projected)


def body(byte_rows, pool_weight, norm_gain, qkv_weight, span_order, query_start):
    local_rows, features = byte_rows.shape
    half_rows = local_rows // 2
    short_rows = local_rows // SF
    span_rows = short_rows // 2
    model_width = qkv_weight.shape[0]
    heads_here = qkv_weight.shape[1]
    head_width = qkv_weight.shape[3]
    width_here = heads_here * head_width
    pair_count = lax.axis_size("seq")
    head_count = lax.axis_size("head")
    seq_index = lax.axis_index("seq")
    head_index = lax.axis_index("head")
    pair_slots = jnp.arange(pair_count, dtype=jnp.int32)
    my_pair = jnp.sum(jnp.where(pair_slots == seq_index, span_order, 0))
    shift_rows = SF - 1
    first_tail = byte_rows[half_rows - shift_rows : half_rows]
    last_tail = byte_rows[local_rows - shift_rows :]
    from_before = lax.ppermute(first_tail, "seq", ring(pair_count, 1))
    from_after = lax.ppermute(last_tail, "seq", ring(pair_count, -1))
    first_prev = jnp.where(my_pair == 0, jnp.zeros_like(from_before), from_before)
    second_prev = jnp.where(my_pair == pair_count - 1, first_tail, from_after)
    grouped = jnp.concatenate(
        [
            first_prev,
            byte_rows[: half_rows - shift_rows],
            second_prev,
            byte_rows[half_rows : local_rows - shift_rows],
        ],
        axis=0,
    )
    grouped = grouped.reshape(short_rows, SF * features)
    partial = jnp.dot(
        grouped, pool_weight.reshape(SF * features, model_width), preferred_element_type=jnp.float32
    )
    sent = partial.astype(jnp.bfloat16)
    total = partial
    for step in range(1, head_count):
        total = total + lax.ppermute(sent, "head", ring(head_count, step)).astype(jnp.float32)
    pooled = total.astype(jnp.bfloat16)
    shortened = lax.dynamic_slice_in_dim(pooled, head_index * features, features, 1)
    widened = pooled.astype(jnp.float32)
    squares = jnp.sum(widened * widened, axis=1, keepdims=True) / model_width
    normed = (widened * lax.rsqrt(squares + norm_epsilon) * norm_gain).astype(jnp.bfloat16)
    projected = jnp.dot(
        normed,
        qkv_weight.reshape(model_width, heads_here * 3 * head_width),
        preferred_element_type=jnp.float32,
    ).astype(jnp.bfloat16)
    window_start = query_start[0]
    from_half = window_start - pair_count * span_rows
    blocks = pair_count * QROWS_DEV // span_rows
    places = from_half // span_rows + jnp.arange(blocks, dtype=jnp.int32)
    rotation = span_order[0]
    first_slots = (2 * pair_count - 1 - places - rotation) % pair_count
    second_slots = (2 * pair_count - 2 - places - rotation) % pair_count
    others = jnp.stack(
        [
            from_half % span_rows,
            my_pair * span_rows,
            (2 * pair_count - 1 - my_pair) * span_rows,
            window_start,
        ]
    )
    numbers = jnp.concatenate([first_slots, second_slots, others]).astype(jnp.int32)
    context, top = attend_all(numbers, projected, pair_count, heads_here, head_width)
    return shortened, context, top[:, :heads_here].T


def solution(mesh):
    placed = (P("seq", "head"), P(None, "head", None), P(), P(None, "head", None, None), P(), P())
    return jax.shard_map(
        body,
        mesh=mesh,
        in_specs=placed,
        out_specs=(P("seq", "head"), P("seq", "head"), P("head", "seq")),
        check_vma=False,
    )
```

```python
import functools

import jax
import jax.numpy as jnp
from jax import lax
from jax.experimental import pallas as pl
from jax.experimental.pallas import tpu as pltpu
from jax.sharding import PartitionSpec as P

SF = 4
QROWS_DEV = 64


norm_epsilon = 1e-06
masked_score = -1e30


LANES = 128
STAT_STEP = 16


def pack_stats(highest, totals):
    high_top = highest.astype(jnp.bfloat16).astype(jnp.float32)
    rest = highest - high_top
    high_mid = rest.astype(jnp.bfloat16).astype(jnp.float32)
    high_low = rest - high_mid
    total_top = totals.astype(jnp.bfloat16).astype(jnp.float32)
    total_low = totals - total_top
    packed = high_top
    for place, piece in enumerate((high_mid, high_low, total_top, total_low)):
        packed = packed + pltpu.roll(piece, STAT_STEP * (place + 1), 1)
    return packed


def unpack_stats(packed):
    def piece(place):
        return pltpu.roll(packed, LANES - STAT_STEP * place, 1)

    return packed + piece(1) + piece(2), piece(3) + piece(4)


def attend_kernel(
    count, head_count, heads, width, numbers, byte_rows, gain, pool_weight, qkv_weight,
    shortened, context, top_out,
    tails, pool_held, qkv_held, own, sent, taken, pooled_all, key_values,
    gathered, parts, arrived,
    load_sem, tail_send, tail_recv, swap_send, swap_recv,
    gather_send, gather_recv, part_send, part_recv,
):
    me = lax.axis_index("seq")
    my_head = lax.axis_index("head")
    core = lax.rem(me, 2)
    middle = lax.rem(me // 2, 2)
    outer = me // 4
    outers = count // 4
    rows = key_values.shape[0]
    span = rows // 2
    total_width = heads * width
    features = byte_rows.shape[1]
    model_width = pool_held.shape[2]
    half_rows = SF * span
    tail_rows = tails.shape[1]
    pool_load = pltpu.make_async_copy(pool_weight, pool_held, load_sem.at[0])
    qkv_load = pltpu.make_async_copy(qkv_weight, qkv_held, load_sem.at[1])
    pool_load.start()
    qkv_load.start()

    def at(outer_at, middle_at, core_at):
        return (lax.rem(outer_at, outers) * 2 + middle_at) * 2 + core_at

    barrier = pltpu.get_barrier_semaphore()

    def greet(step, carry):
        pl.semaphore_signal(
            barrier, inc=1, device_id={"seq": lax.rem(me + step, count)},
            device_id_type=pl.DeviceIdType.MESH,
        )
        return carry

    lax.fori_loop(1, count, greet, 0)
    def greet_head(step, carry):
        pl.semaphore_signal(
            barrier, inc=1, device_id={"head": lax.rem(my_head + step, head_count)},
            device_id_type=pl.DeviceIdType.MESH,
        )
        return carry

    lax.fori_loop(1, head_count, greet_head, 0)
    pl.semaphore_wait(barrier, count - 1 + head_count - 1)

    def tail_copy(place, target):
        end = half_rows * (place + 1)
        return pltpu.make_async_remote_copy(
            src_ref=byte_rows.at[end - tail_rows : end], dst_ref=tails.at[place],
            send_sem=tail_send.at[place], recv_sem=tail_recv.at[place],
            device_id={"seq": target}, device_id_type=pl.DeviceIdType.MESH,
        )

    tail_copies = [
        tail_copy(0, lax.rem(me + 1, count)), tail_copy(1, lax.rem(me + count - 1, count))
    ]
    tail_copies[1].start()
    tail_copies[0].start()
    pool_row = lax.broadcasted_iota(jnp.int32, (span, half_rows), 0)
    pool_col = lax.broadcasted_iota(jnp.int32, (span, half_rows), 1)
    out_row = lax.broadcasted_iota(jnp.int32, (span, features), 0)

    def swap_copy(half, step):
        target = lax.rem(my_head + step, head_count)
        return pltpu.make_async_remote_copy(
            src_ref=sent.at[half], dst_ref=taken.at[my_head, half],
            send_sem=swap_send.at[step, half], recv_sem=swap_recv.at[my_head, half],
            device_id={"head": target}, device_id_type=pl.DeviceIdType.MESH,
        )

    def pool(half, before):
        block = byte_rows[half * half_rows : (half + 1) * half_rows, :]
        total = jnp.zeros((span, model_width), jnp.float32)
        for shift in range(SF):
            chosen = pool_col == SF * pool_row + (shift - SF + 1)
            chosen = jnp.where(chosen, 1.0, 0.0).astype(jnp.bfloat16)
            picked = jnp.dot(chosen, block, preferred_element_type=jnp.float32)
            if shift < SF - 1:
                at_row = tail_rows - SF + 1 + shift
                picked = jnp.where(out_row == 0, before[at_row : at_row + 1], picked)
            total = total + jnp.dot(
                picked.astype(jnp.bfloat16), pool_held[shift], preferred_element_type=jnp.float32
            )
        own[half] = total
        sent[half] = total.astype(jnp.bfloat16)
        for step in range(1, head_count):
            swap_copy(half, step).start()

    def normed_half(half):
        total = own[half]
        for step in range(1, head_count):
            source = lax.rem(my_head + step, head_count)
            pltpu.make_async_remote_copy(
                src_ref=sent.at[half], dst_ref=taken.at[source, half],
                send_sem=swap_send.at[step, half], recv_sem=swap_recv.at[source, half],
                device_id={"head": source}, device_id_type=pl.DeviceIdType.MESH,
            ).wait_recv()
            total = total + taken[source, half].astype(jnp.float32)
        pooled = total.astype(jnp.bfloat16)
        pooled_all[half * span : (half + 1) * span, :] = pooled
        widened = pooled.astype(jnp.float32)
        squares = jnp.sum(widened * widened, axis=1, keepdims=True) / model_width
        return (widened * lax.rsqrt(squares + norm_epsilon) * gain[...]).astype(jnp.bfloat16)

    def project_half(half, normed):
        key_values[half * span : (half + 1) * span, :] = jnp.dot(
            normed, qkv_held[:, total_width:], preferred_element_type=jnp.float32
        ).astype(jnp.bfloat16)

    pair_base = numbers[count + 1]
    own_tail = byte_rows[half_rows - tail_rows : half_rows, :].astype(jnp.float32)
    pool_load.wait()
    tail_copies[1].wait_recv()
    pool(
        1, jnp.where(pair_base == (count - 1) * span, own_tail, tails[1].astype(jnp.float32))
    )
    tail_copies[0].wait_recv()
    pool(0, jnp.where(pair_base == 0, 0.0, tails[0].astype(jnp.float32)))
    qkv_load.wait()
    late_normed = normed_half(1)
    gathered[me] = jnp.dot(
        late_normed, qkv_held[:, :total_width], preferred_element_type=jnp.float32
    ).astype(jnp.bfloat16)

    pushes = []

    def push(slot, target):
        copy = pltpu.make_async_remote_copy(
            src_ref=gathered.at[slot], dst_ref=gathered.at[slot],
            send_sem=gather_send.at[len(pushes)], recv_sem=gather_recv.at[slot],
            device_id={"seq": target}, device_id_type=pl.DeviceIdType.MESH,
        )
        copy.start()
        pushes.append(copy)

    def landed(slot):
        pltpu.make_async_remote_copy(
            src_ref=gathered.at[slot], dst_ref=gathered.at[slot],
            send_sem=gather_send.at[0], recv_sem=gather_recv.at[slot],
            device_id={"seq": at(outer, middle, 1 - core)},
            device_id_type=pl.DeviceIdType.MESH,
        ).wait_recv()

    across = at(outer, 1 - middle, core)
    sibling = at(outer, middle, 1 - core)
    for step in range(1, outers):
        push(me, at(outer + step, middle, core))
    push(me, across)
    push(me, sibling)
    project_half(1, late_normed)
    project_half(0, normed_half(0))
    shortened[...] = pooled_all[
        :, pl.ds(pl.multiple_of(my_head * features, LANES), features)
    ]
    for step in range(1, outers):
        slot = at(outer + step, middle, core)
        landed(slot)
        push(slot, across)
        push(slot, sibling)
    for step in range(outers):
        slot = at(outer + step, 1 - middle, core)
        landed(slot)
        push(slot, sibling)
    for step in range(outers):
        landed(at(outer + step, middle, 1 - core))
        landed(at(outer + step, 1 - middle, 1 - core))

    blocks = count // 2
    offset = numbers[2 * blocks]
    first_base = numbers[2 * blocks + 1]
    second_base = numbers[2 * blocks + 2]
    window_start = numbers[2 * blocks + 3]
    pick_row = lax.broadcasted_iota(jnp.int32, (span, 2 * span), 0)
    pick_col = lax.broadcasted_iota(jnp.int32, (span, 2 * span), 1)
    pick = jnp.where(pick_col == pick_row + offset, 1.0, 0.0).astype(jnp.bfloat16)
    key_col = lax.broadcasted_iota(jnp.int32, (span, rows), 1)
    key_pos = jnp.where(key_col < span, first_base + key_col, second_base + key_col - span)
    ahead = key_pos - lax.broadcasted_iota(jnp.int32, (span, rows), 0) - window_start
    lane = lax.broadcasted_iota(jnp.int32, (span, LANES), 1)
    scale = width ** (-0.5)

    def part_copy(target):
        return pltpu.make_async_remote_copy(
            src_ref=parts.at[target], dst_ref=arrived.at[me],
            send_sem=part_send.at[target], recv_sem=part_recv.at[me],
            device_id={"seq": target}, device_id_type=pl.DeviceIdType.MESH,
        )

    def attend(step, carry):
        block = lax.rem(me // 2 + 1 + step, blocks)
        both = jnp.concatenate(
            [gathered[numbers[block]], gathered[numbers[blocks + block]]], axis=0
        )
        queries = jnp.dot(pick, both, preferred_element_type=jnp.float32).astype(jnp.bfloat16)
        allowed = ahead <= block * span
        highs = jnp.zeros((span, LANES), jnp.float32)
        totals = jnp.zeros((span, LANES), jnp.float32)
        for head in range(heads):
            base = head * width
            keys = key_values[:, base : base + width]
            values = key_values[:, total_width + base : total_width + base + width]
            scores = lax.dot_general(
                queries[:, head * width : (head + 1) * width], keys,
                (((1,), (1,)), ((), ())), preferred_element_type=jnp.float32,
            ) * scale
            scores = jnp.where(allowed, scores, masked_score)
            high = jnp.max(scores, axis=1, keepdims=True)
            weights = jnp.exp(scores - high).astype(jnp.bfloat16)
            total = jnp.sum(weights.astype(jnp.float32), axis=1, keepdims=True)
            summed = jnp.dot(weights, values, preferred_element_type=jnp.float32)
            summed = summed.astype(jnp.bfloat16)
            columns = slice(head * width, (head + 1) * width)
            parts[2 * block, :, columns] = summed[: span // 2]
            parts[2 * block + 1, :, columns] = summed[span // 2 :]
            highs = jnp.where(lane == head, high, highs)
            totals = jnp.where(lane == head, total, totals)
        packed = pack_stats(highs, totals).astype(jnp.bfloat16)
        parts[2 * block, :, total_width:] = packed[: span // 2]
        parts[2 * block + 1, :, total_width:] = packed[span // 2 :]
        for side in range(2):
            target = 2 * block + side

            @pl.when(target != me)
            def _():
                part_copy(target).start()

        return carry

    lax.fori_loop(0, blocks, attend, 0)
    arrived[me] = parts[me]

    def settle(step, carry):
        source = lax.rem(me + step, count)
        pltpu.make_async_remote_copy(
            src_ref=parts.at[source], dst_ref=arrived.at[source],
            send_sem=part_send.at[source], recv_sem=part_recv.at[source],
            device_id={"seq": source}, device_id_type=pl.DeviceIdType.MESH,
        ).wait()
        return carry

    lax.fori_loop(1, count, settle, 0)
    for copy in pushes:
        copy.wait_send()
    for copy in tail_copies:
        copy.wait_send()
    for half in range(2):
        for step in range(1, head_count):
            swap_copy(half, step).wait_send()

    def stats_of(source):
        return unpack_stats(arrived[source, :, total_width:].astype(jnp.float32))

    top = lax.fori_loop(
        1, count, lambda source, best: jnp.maximum(best, stats_of(source)[0]), stats_of(0)[0]
    )
    def add(source, carry):
        denominator, pieces = carry
        highs, totals = stats_of(source)
        factor = jnp.exp(highs - top)
        pieces = tuple(
            pieces[head]
            + arrived[source, :, head * width : (head + 1) * width].astype(jnp.float32)
            * factor[:, head : head + 1]
            for head in range(heads)
        )
        return denominator + factor * totals, pieces

    empty = jnp.zeros((span // 2, width), jnp.float32)
    denominator, pieces = lax.fori_loop(
        0, count, add, (jnp.zeros((span // 2, LANES), jnp.float32), (empty,) * heads)
    )
    for head in range(heads):
        context[:, head * width : (head + 1) * width] = (
            pieces[head] / denominator[:, head : head + 1]
        ).astype(jnp.bfloat16)
    top_out[...] = top * width**0.5


def whole_kernel(numbers, byte_rows, gain, pool_weight, qkv_weight, count, head_count, heads, width):
    span = byte_rows.shape[0] // (2 * SF)
    features = byte_rows.shape[1]
    model_width = pool_weight.shape[2]
    total_width = heads * width
    vmem = pl.BlockSpec(memory_space=pltpu.VMEM)
    return pl.pallas_call(
        functools.partial(attend_kernel, count, head_count, heads, width),
        out_shape=(
            jax.ShapeDtypeStruct((2 * span, features), jnp.bfloat16),
            jax.ShapeDtypeStruct((span // 2, total_width), jnp.bfloat16),
            jax.ShapeDtypeStruct((span // 2, LANES), jnp.float32),
        ),
        in_specs=[
            pl.BlockSpec(memory_space=pltpu.SMEM),
            vmem,
            vmem,
            pl.BlockSpec(memory_space=pl.ANY),
            pl.BlockSpec(memory_space=pl.ANY),
        ],
        out_specs=(vmem, vmem, vmem),
        scratch_shapes=[
            pltpu.VMEM((2, 16, features), jnp.bfloat16),
            pltpu.VMEM(pool_weight.shape, jnp.bfloat16),
            pltpu.VMEM(qkv_weight.shape, jnp.bfloat16),
            pltpu.VMEM((2, span, model_width), jnp.float32),
            pltpu.VMEM((2, span, model_width), jnp.bfloat16),
            pltpu.VMEM((head_count, 2, span, model_width), jnp.bfloat16),
            pltpu.VMEM((2 * span, model_width), jnp.bfloat16),
            pltpu.VMEM((2 * span, 2 * total_width), jnp.bfloat16),
            pltpu.VMEM((count, span, total_width), jnp.bfloat16),
            pltpu.VMEM((count, span // 2, total_width + LANES), jnp.bfloat16),
            pltpu.VMEM((count, span // 2, total_width + LANES), jnp.bfloat16),
            pltpu.SemaphoreType.DMA((2,)),
            pltpu.SemaphoreType.DMA((2,)),
            pltpu.SemaphoreType.DMA((2,)),
            pltpu.SemaphoreType.DMA((head_count, 2)),
            pltpu.SemaphoreType.DMA((head_count, 2)),
            pltpu.SemaphoreType.DMA((count,)),
            pltpu.SemaphoreType.DMA((count,)),
            pltpu.SemaphoreType.DMA((count,)),
            pltpu.SemaphoreType.DMA((count,)),
        ],
        compiler_params=pltpu.CompilerParams(
            collective_id=0, has_side_effects=True, vmem_limit_bytes=48 * 1024 * 1024
        ),
    )(numbers, byte_rows, gain, pool_weight, qkv_weight)


def body(byte_rows, pool_weight, norm_gain, qkv_weight, span_order, query_start):
    span_rows = byte_rows.shape[0] // (2 * SF)
    model_width, heads_here, _, head_width = qkv_weight.shape
    pair_count = lax.axis_size("seq")
    head_count = lax.axis_size("head")
    pair_slots = jnp.arange(pair_count, dtype=jnp.int32)
    my_pair = jnp.sum(jnp.where(pair_slots == lax.axis_index("seq"), span_order, 0))
    window_start = query_start[0]
    from_half = window_start - pair_count * span_rows
    blocks = pair_count * QROWS_DEV // span_rows
    places = from_half // span_rows + jnp.arange(blocks, dtype=jnp.int32)
    rotation = span_order[0]
    first_slots = (2 * pair_count - 1 - places - rotation) % pair_count
    second_slots = (2 * pair_count - 2 - places - rotation) % pair_count
    others = jnp.stack(
        [
            from_half % span_rows,
            my_pair * span_rows,
            (2 * pair_count - 1 - my_pair) * span_rows,
            window_start,
        ]
    )
    numbers = jnp.concatenate([first_slots, second_slots, others]).astype(jnp.int32)
    qkv_flat = qkv_weight.transpose(0, 2, 1, 3).reshape(model_width, -1)
    shortened, context, top = whole_kernel(
        numbers, byte_rows, norm_gain.reshape(1, -1), pool_weight, qkv_flat,
        pair_count, head_count, heads_here, head_width,
    )
    return shortened, context, top[:, :heads_here].T


def solution(mesh):
    placed = (P("seq", "head"), P(None, "head", None), P(), P(None, "head", None, None), P(), P())
    return jax.shard_map(
        body,
        mesh=mesh,
        in_specs=placed,
        out_specs=(P("seq", "head"), P("seq", "head"), P("head", "seq")),
        check_vma=False,
    )
```

```python
import functools

import jax
import jax.numpy as jnp
from jax import lax
from jax.experimental import pallas as pl
from jax.experimental.pallas import tpu as pltpu
from jax.sharding import PartitionSpec as P

SF = 4


norm_epsilon = 1e-06
masked_score = -1e30


LANES = 128
STAT_STEP = 16


def pack_stats(highest, totals):
    high_top = highest.astype(jnp.bfloat16).astype(jnp.float32)
    rest = highest - high_top
    high_mid = rest.astype(jnp.bfloat16).astype(jnp.float32)
    high_low = rest - high_mid
    total_top = totals.astype(jnp.bfloat16).astype(jnp.float32)
    total_low = totals - total_top
    packed = high_top
    for place, piece in enumerate((high_mid, high_low, total_top, total_low)):
        packed = packed + pltpu.roll(piece, STAT_STEP * (place + 1), 1)
    return packed


def unpack_stats(packed):
    def piece(place):
        return pltpu.roll(packed, LANES - STAT_STEP * place, 1)

    return packed + piece(1) + piece(2), piece(3) + piece(4)


def attend_kernel(
    count, head_count, heads, width, span_order, query_start, byte_rows, gain, pool_weight, qkv_weight,
    shortened, context, top_out,
    tails, pool_held, qkv_held, own, sent, taken, pooled_all, key_values,
    gathered, parts, given, merged, arrived,
    load_sem, tail_send, tail_recv, swap_send, swap_recv,
    gather_send, gather_recv, give_send, give_recv, part_send, part_recv,
):
    me = lax.axis_index("seq")
    my_head = lax.axis_index("head")
    core = lax.rem(me, 2)
    middle = lax.rem(me // 2, 2)
    outer = me // 4
    outers = count // 4
    rows = key_values.shape[0]
    span = rows // 2
    total_width = heads * width
    features = byte_rows.shape[1]
    model_width = pool_held.shape[2]
    half_rows = SF * span
    tail_rows = tails.shape[1]
    pool_load = pltpu.make_async_copy(pool_weight, pool_held, load_sem.at[0])
    qkv_load = pltpu.make_async_copy(qkv_weight, qkv_held, load_sem.at[1])
    pool_load.start()
    qkv_load.start()

    def at(outer_at, middle_at, core_at):
        return (lax.rem(outer_at, outers) * 2 + middle_at) * 2 + core_at

    barrier = pltpu.get_barrier_semaphore()

    def greet(step, carry):
        pl.semaphore_signal(
            barrier, inc=1, device_id={"seq": lax.rem(me + step, count)},
            device_id_type=pl.DeviceIdType.MESH,
        )
        return carry

    lax.fori_loop(1, count, greet, 0)
    def greet_head(step, carry):
        pl.semaphore_signal(
            barrier, inc=1, device_id={"head": lax.rem(my_head + step, head_count)},
            device_id_type=pl.DeviceIdType.MESH,
        )
        return carry

    lax.fori_loop(1, head_count, greet_head, 0)
    pl.semaphore_wait(barrier, count - 1 + head_count - 1)

    def tail_copy(place, target):
        end = half_rows * (place + 1)
        return pltpu.make_async_remote_copy(
            src_ref=byte_rows.at[end - tail_rows : end], dst_ref=tails.at[place],
            send_sem=tail_send.at[place], recv_sem=tail_recv.at[place],
            device_id={"seq": target}, device_id_type=pl.DeviceIdType.MESH,
        )

    tail_copies = [
        tail_copy(0, lax.rem(me + 1, count)), tail_copy(1, lax.rem(me + count - 1, count))
    ]
    tail_copies[1].start()
    tail_copies[0].start()
    pool_row = lax.broadcasted_iota(jnp.int32, (span, half_rows), 0)
    pool_col = lax.broadcasted_iota(jnp.int32, (span, half_rows), 1)
    out_row = lax.broadcasted_iota(jnp.int32, (span, features), 0)

    def swap_copy(half, step):
        target = lax.rem(my_head + step, head_count)
        return pltpu.make_async_remote_copy(
            src_ref=sent.at[half], dst_ref=taken.at[my_head, half],
            send_sem=swap_send.at[step, half], recv_sem=swap_recv.at[my_head, half],
            device_id={"head": target}, device_id_type=pl.DeviceIdType.MESH,
        )

    def pool(half, before):
        block = byte_rows[half * half_rows : (half + 1) * half_rows, :]
        total = jnp.zeros((span, model_width), jnp.float32)
        for shift in range(SF):
            chosen = pool_col == SF * pool_row + (shift - SF + 1)
            chosen = jnp.where(chosen, 1.0, 0.0).astype(jnp.bfloat16)
            picked = jnp.dot(chosen, block, preferred_element_type=jnp.float32)
            if shift < SF - 1:
                at_row = tail_rows - SF + 1 + shift
                picked = jnp.where(out_row == 0, before[at_row : at_row + 1], picked)
            total = total + jnp.dot(
                picked.astype(jnp.bfloat16), pool_held[shift], preferred_element_type=jnp.float32
            )
        own[half] = total
        sent[half] = total.astype(jnp.bfloat16)
        for step in range(1, head_count):
            swap_copy(half, step).start()

    def normed_half(half):
        total = own[half]
        for step in range(1, head_count):
            source = lax.rem(my_head + step, head_count)
            pltpu.make_async_remote_copy(
                src_ref=sent.at[half], dst_ref=taken.at[source, half],
                send_sem=swap_send.at[step, half], recv_sem=swap_recv.at[source, half],
                device_id={"head": source}, device_id_type=pl.DeviceIdType.MESH,
            ).wait_recv()
            total = total + taken[source, half].astype(jnp.float32)
        pooled = total.astype(jnp.bfloat16)
        pooled_all[half * span : (half + 1) * span, :] = pooled
        widened = pooled.astype(jnp.float32)
        squares = jnp.sum(widened * widened, axis=1, keepdims=True) / model_width
        return (widened * lax.rsqrt(squares + norm_epsilon) * gain[...]).astype(jnp.bfloat16)

    def project_half(half, normed):
        key_values[half * span : (half + 1) * span, :] = jnp.dot(
            normed, qkv_held[:, total_width:], preferred_element_type=jnp.float32
        ).astype(jnp.bfloat16)

    pair_base = span_order[me] * span
    own_tail = byte_rows[half_rows - tail_rows : half_rows, :].astype(jnp.float32)
    pool_load.wait()
    tail_copies[1].wait_recv()
    pool(
        1, jnp.where(pair_base == (count - 1) * span, own_tail, tails[1].astype(jnp.float32))
    )
    tail_copies[0].wait_recv()
    pool(0, jnp.where(pair_base == 0, 0.0, tails[0].astype(jnp.float32)))
    qkv_load.wait()
    late_normed = normed_half(1)
    gathered[me] = jnp.dot(
        late_normed, qkv_held[:, :total_width], preferred_element_type=jnp.float32
    ).astype(jnp.bfloat16)

    pushes = []

    def push(slot, target):
        copy = pltpu.make_async_remote_copy(
            src_ref=gathered.at[slot], dst_ref=gathered.at[slot],
            send_sem=gather_send.at[len(pushes)], recv_sem=gather_recv.at[slot],
            device_id={"seq": target}, device_id_type=pl.DeviceIdType.MESH,
        )
        copy.start()
        pushes.append(copy)

    def landed(slot):
        pltpu.make_async_remote_copy(
            src_ref=gathered.at[slot], dst_ref=gathered.at[slot],
            send_sem=gather_send.at[0], recv_sem=gather_recv.at[slot],
            device_id={"seq": at(outer, middle, 1 - core)},
            device_id_type=pl.DeviceIdType.MESH,
        ).wait_recv()

    across = at(outer, 1 - middle, core)
    sibling = at(outer, middle, 1 - core)
    for step in range(1, outers):
        push(me, at(outer + step, middle, core))
    push(me, across)
    push(me, sibling)
    project_half(1, late_normed)
    project_half(0, normed_half(0))
    shortened[...] = pooled_all[
        :, pl.ds(pl.multiple_of(my_head * features, LANES), features)
    ]
    for step in range(1, outers):
        slot = at(outer + step, middle, core)
        landed(slot)
        push(slot, across)
        push(slot, sibling)
    for step in range(outers):
        slot = at(outer + step, 1 - middle, core)
        landed(slot)
        push(slot, sibling)
    for step in range(outers):
        landed(at(outer + step, middle, 1 - core))
        landed(at(outer + step, 1 - middle, 1 - core))

    blocks = count // 2
    chip = me // 2
    window_start = query_start[0]
    from_half = window_start - count * span
    first_place = lax.div(from_half, span)
    offset = from_half - first_place * span
    slot_base = 2 * count - 1 - first_place - span_order[0]
    first_base = pair_base
    second_base = (2 * count - 1) * span - pair_base
    pick_row = lax.broadcasted_iota(jnp.int32, (span, 2 * span), 0)
    pick_col = lax.broadcasted_iota(jnp.int32, (span, 2 * span), 1)
    pick = jnp.where(pick_col == pick_row + offset, 1.0, 0.0).astype(jnp.bfloat16)
    key_col = lax.broadcasted_iota(jnp.int32, (span, rows), 1)
    key_pos = jnp.where(key_col < span, first_base + key_col, second_base + key_col - span)
    ahead = key_pos - lax.broadcasted_iota(jnp.int32, (span, rows), 0) - window_start
    lane = lax.broadcasted_iota(jnp.int32, (span, LANES), 1)
    scale = width ** (-0.5)

    half_lane = lax.broadcasted_iota(jnp.int32, (span // 2, LANES), 1)

    def block_at(step):
        return lax.rem(chip + 1 + step, blocks)

    def give_copy(block):
        return pltpu.make_async_remote_copy(
            src_ref=parts.at[2 * block + 1 - core], dst_ref=given.at[block],
            send_sem=give_send.at[block], recv_sem=give_recv.at[block],
            device_id={"seq": sibling}, device_id_type=pl.DeviceIdType.MESH,
        )

    def part_copy(block, source):
        return pltpu.make_async_remote_copy(
            src_ref=merged.at[block], dst_ref=arrived.at[source],
            send_sem=part_send.at[block], recv_sem=part_recv.at[source],
            device_id={"seq": 2 * block + core}, device_id_type=pl.DeviceIdType.MESH,
        )

    def merge(block, into, place):
        give_copy(block).wait_recv()
        mine = 2 * block + core
        my_highs, my_totals = unpack_stats(parts[mine, :, total_width:].astype(jnp.float32))
        highs, totals = unpack_stats(given[block, :, total_width:].astype(jnp.float32))
        best = jnp.maximum(my_highs, highs)
        my_factor = jnp.exp(my_highs - best)
        factor = jnp.exp(highs - best)
        total = my_totals * my_factor + totals * factor
        for head in range(heads):
            columns = slice(head * width, (head + 1) * width)
            into[place, :, columns] = (
                parts[mine, :, columns].astype(jnp.float32) * my_factor[:, head : head + 1]
                + given[block, :, columns].astype(jnp.float32) * factor[:, head : head + 1]
            ).astype(jnp.bfloat16)
        used = half_lane < heads
        into[place, :, total_width:] = pack_stats(
            jnp.where(used, best, 0.0), jnp.where(used, total, 0.0)
        ).astype(jnp.bfloat16)

    def attend(step, carry):
        block = block_at(step)
        both = jnp.concatenate(
            [
                gathered[lax.rem(slot_base - block, count)],
                gathered[lax.rem(slot_base - block - 1, count)],
            ], axis=0
        )
        queries = jnp.dot(pick, both, preferred_element_type=jnp.float32).astype(jnp.bfloat16)
        allowed = ahead <= block * span
        highs = jnp.zeros((span, LANES), jnp.float32)
        totals = jnp.zeros((span, LANES), jnp.float32)
        for head in range(heads):
            base = head * width
            keys = key_values[:, base : base + width]
            values = key_values[:, total_width + base : total_width + base + width]
            scores = lax.dot_general(
                queries[:, head * width : (head + 1) * width], keys,
                (((1,), (1,)), ((), ())), preferred_element_type=jnp.float32,
            ) * scale
            scores = jnp.where(allowed, scores, masked_score)
            high = jnp.max(scores, axis=1, keepdims=True)
            weights = jnp.exp(scores - high).astype(jnp.bfloat16)
            total = jnp.sum(weights.astype(jnp.float32), axis=1, keepdims=True)
            summed = jnp.dot(weights, values, preferred_element_type=jnp.float32)
            summed = summed.astype(jnp.bfloat16)
            columns = slice(head * width, (head + 1) * width)
            parts[2 * block, :, columns] = summed[: span // 2]
            parts[2 * block + 1, :, columns] = summed[span // 2 :]
            highs = jnp.where(lane == head, high, highs)
            totals = jnp.where(lane == head, total, totals)
        packed = pack_stats(highs, totals).astype(jnp.bfloat16)
        parts[2 * block, :, total_width:] = packed[: span // 2]
        parts[2 * block + 1, :, total_width:] = packed[span // 2 :]
        give_copy(block).start()

        @pl.when(step > 0)
        def _():
            before = block_at(step - 1)
            merge(before, merged, before)
            part_copy(before, chip).start()

        return carry

    lax.fori_loop(0, blocks, attend, 0)
    merge(chip, arrived, chip)

    def settle(step, carry):
        other = lax.rem(chip + step, blocks)
        part_copy(other, chip).wait_send()
        part_copy(other, other).wait_recv()
        return carry

    lax.fori_loop(1, blocks, settle, 0)

    def given_away(block, carry):
        give_copy(block).wait_send()
        return carry

    lax.fori_loop(0, blocks, given_away, 0)
    for copy in pushes:
        copy.wait_send()
    for copy in tail_copies:
        copy.wait_send()
    for half in range(2):
        for step in range(1, head_count):
            swap_copy(half, step).wait_send()

    def stats_of(source):
        return unpack_stats(arrived[source, :, total_width:].astype(jnp.float32))

    top = lax.fori_loop(
        1, blocks, lambda source, best: jnp.maximum(best, stats_of(source)[0]), stats_of(0)[0]
    )
    def add(source, carry):
        denominator, pieces = carry
        highs, totals = stats_of(source)
        factor = jnp.exp(highs - top)
        pieces = tuple(
            pieces[head]
            + arrived[source, :, head * width : (head + 1) * width].astype(jnp.float32)
            * factor[:, head : head + 1]
            for head in range(heads)
        )
        return denominator + factor * totals, pieces

    empty = jnp.zeros((span // 2, width), jnp.float32)
    denominator, pieces = lax.fori_loop(
        0, blocks, add, (jnp.zeros((span // 2, LANES), jnp.float32), (empty,) * heads)
    )
    for head in range(heads):
        context[:, head * width : (head + 1) * width] = (
            pieces[head] / denominator[:, head : head + 1]
        ).astype(jnp.bfloat16)
    turned = jnp.concatenate([top, top], axis=0).T
    top_out[...] = turned[:heads, : span // 2] * width**0.5


def whole_kernel(
    span_order, query_start, byte_rows, gain, pool_weight, qkv_weight, count, head_count, heads, width
):
    span = byte_rows.shape[0] // (2 * SF)
    features = byte_rows.shape[1]
    model_width = pool_weight.shape[2]
    total_width = heads * width
    vmem = pl.BlockSpec(memory_space=pltpu.VMEM)
    return pl.pallas_call(
        functools.partial(attend_kernel, count, head_count, heads, width),
        out_shape=(
            jax.ShapeDtypeStruct((2 * span, features), jnp.bfloat16),
            jax.ShapeDtypeStruct((span // 2, total_width), jnp.bfloat16),
            jax.ShapeDtypeStruct((heads, span // 2), jnp.float32),
        ),
        in_specs=[
            pl.BlockSpec(memory_space=pltpu.SMEM),
            pl.BlockSpec(memory_space=pltpu.SMEM),
            vmem,
            vmem,
            pl.BlockSpec(memory_space=pl.ANY),
            pl.BlockSpec(memory_space=pl.ANY),
        ],
        out_specs=(vmem, vmem, vmem),
        scratch_shapes=[
            pltpu.VMEM((2, 16, features), jnp.bfloat16),
            pltpu.VMEM(pool_weight.shape, jnp.bfloat16),
            pltpu.VMEM(qkv_weight.shape, jnp.bfloat16),
            pltpu.VMEM((2, span, model_width), jnp.float32),
            pltpu.VMEM((2, span, model_width), jnp.bfloat16),
            pltpu.VMEM((head_count, 2, span, model_width), jnp.bfloat16),
            pltpu.VMEM((2 * span, model_width), jnp.bfloat16),
            pltpu.VMEM((2 * span, 2 * total_width), jnp.bfloat16),
            pltpu.VMEM((count, span, total_width), jnp.bfloat16),
            pltpu.VMEM((count, span // 2, total_width + LANES), jnp.bfloat16),
            pltpu.VMEM((count // 2, span // 2, total_width + LANES), jnp.bfloat16),
            pltpu.VMEM((count // 2, span // 2, total_width + LANES), jnp.bfloat16),
            pltpu.VMEM((count // 2, span // 2, total_width + LANES), jnp.bfloat16),
            pltpu.SemaphoreType.DMA((2,)),
            pltpu.SemaphoreType.DMA((2,)),
            pltpu.SemaphoreType.DMA((2,)),
            pltpu.SemaphoreType.DMA((head_count, 2)),
            pltpu.SemaphoreType.DMA((head_count, 2)),
            pltpu.SemaphoreType.DMA((count,)),
            pltpu.SemaphoreType.DMA((count,)),
            pltpu.SemaphoreType.DMA((count // 2,)),
            pltpu.SemaphoreType.DMA((count // 2,)),
            pltpu.SemaphoreType.DMA((count // 2,)),
            pltpu.SemaphoreType.DMA((count // 2,)),
        ],
        compiler_params=pltpu.CompilerParams(
            collective_id=0, has_side_effects=True, vmem_limit_bytes=48 * 1024 * 1024
        ),
    )(span_order, query_start, byte_rows, gain, pool_weight, qkv_weight)


def body(byte_rows, pool_weight, norm_gain, qkv_weight, span_order, query_start):
    model_width, heads_here, _, head_width = qkv_weight.shape
    qkv_flat = qkv_weight.transpose(0, 2, 1, 3).reshape(model_width, -1)
    return whole_kernel(
        span_order, query_start, byte_rows, norm_gain.reshape(1, -1), pool_weight, qkv_flat,
        lax.axis_size("seq"), lax.axis_size("head"), heads_here, head_width,
    )


def solution(mesh):
    placed = (P("seq", "head"), P(None, "head", None), P(), P(None, "head", None, None), P(), P())
    return jax.shard_map(
        body,
        mesh=mesh,
        in_specs=placed,
        out_specs=(P("seq", "head"), P("seq", "head"), P("head", "seq")),
        check_vma=False,
    )
```

```python
import functools

import jax
import jax.numpy as jnp
from jax import lax
from jax.experimental import pallas as pl
from jax.experimental.pallas import tpu as pltpu
from jax.sharding import PartitionSpec as P

SF = 4


norm_epsilon = 1e-06
masked_score = -1e30


LANES = 128
STAT_STEP = 16


def pack_stats(highest, totals):
    high_top = highest.astype(jnp.bfloat16).astype(jnp.float32)
    rest = highest - high_top
    high_mid = rest.astype(jnp.bfloat16).astype(jnp.float32)
    high_low = rest - high_mid
    total_top = totals.astype(jnp.bfloat16).astype(jnp.float32)
    total_low = totals - total_top
    packed = high_top
    for place, piece in enumerate((high_mid, high_low, total_top, total_low)):
        packed = packed + pltpu.roll(piece, STAT_STEP * (place + 1), 1)
    return packed


def unpack_stats(packed):
    def piece(place):
        return pltpu.roll(packed, LANES - STAT_STEP * place, 1)

    return packed + piece(1) + piece(2), piece(3) + piece(4)


def attend_kernel(
    count, head_count, heads, width, span_order, query_start, rows_in, gain, pool_weight, qkv_weight,
    shortened, context, top_out,
    byte_rows, tails, pool_held, qkv_held, own, sent, taken, pooled_all, key_values,
    gathered, parts, given, merged, arrived,
    load_sem, tail_send, tail_recv, swap_send, swap_recv,
    gather_send, gather_recv, give_send, give_recv, part_send, part_recv,
):
    me = lax.axis_index("seq")
    my_head = lax.axis_index("head")
    core = lax.rem(me, 2)
    middle = lax.rem(me // 2, 2)
    outer = me // 4
    outers = count // 4
    rows = key_values.shape[0]
    span = rows // 2
    total_width = heads * width
    features = byte_rows.shape[1]
    model_width = pool_held.shape[2]
    half_rows = SF * span
    tail_rows = tails.shape[1]
    pool_load = pltpu.make_async_copy(pool_weight, pool_held, load_sem.at[0])
    qkv_load = pltpu.make_async_copy(qkv_weight, qkv_held, load_sem.at[1])
    rows_load = pltpu.make_async_copy(rows_in, byte_rows, load_sem.at[2])
    rows_load.start()
    pool_load.start()
    qkv_load.start()

    def at(outer_at, middle_at, core_at):
        return (lax.rem(outer_at, outers) * 2 + middle_at) * 2 + core_at

    barrier = pltpu.get_barrier_semaphore()

    def greet(step, carry):
        pl.semaphore_signal(
            barrier, inc=1, device_id={"seq": lax.rem(me + step, count)},
            device_id_type=pl.DeviceIdType.MESH,
        )
        return carry

    lax.fori_loop(1, count, greet, 0)
    def greet_head(step, carry):
        pl.semaphore_signal(
            barrier, inc=1, device_id={"head": lax.rem(my_head + step, head_count)},
            device_id_type=pl.DeviceIdType.MESH,
        )
        return carry

    lax.fori_loop(1, head_count, greet_head, 0)
    pool_row = lax.broadcasted_iota(jnp.int32, (span, half_rows), 0)
    pool_col = lax.broadcasted_iota(jnp.int32, (span, half_rows), 1)
    out_row = lax.broadcasted_iota(jnp.int32, (span, features), 0)

    def pick_rows(half):
        block = byte_rows[half * half_rows : (half + 1) * half_rows, :]
        picks = []
        for shift in range(SF):
            chosen = pool_col == SF * pool_row + (shift - SF + 1)
            chosen = jnp.where(chosen, 1.0, 0.0).astype(jnp.bfloat16)
            picks.append(jnp.dot(chosen, block, preferred_element_type=jnp.float32))
        return picks

    rows_load.wait()
    late_picks = pick_rows(1)
    pl.semaphore_wait(barrier, count - 1 + head_count - 1)

    def tail_copy(place, target):
        end = half_rows * (place + 1)
        return pltpu.make_async_remote_copy(
            src_ref=byte_rows.at[end - tail_rows : end], dst_ref=tails.at[place],
            send_sem=tail_send.at[place], recv_sem=tail_recv.at[place],
            device_id={"seq": target}, device_id_type=pl.DeviceIdType.MESH,
        )

    tail_copies = [
        tail_copy(0, lax.rem(me + 1, count)), tail_copy(1, lax.rem(me + count - 1, count))
    ]
    tail_copies[1].start()
    tail_copies[0].start()
    def swap_copy(half, step):
        target = lax.rem(my_head + step, head_count)
        return pltpu.make_async_remote_copy(
            src_ref=sent.at[half], dst_ref=taken.at[my_head, half],
            send_sem=swap_send.at[step, half], recv_sem=swap_recv.at[my_head, half],
            device_id={"head": target}, device_id_type=pl.DeviceIdType.MESH,
        )

    def pool(half, picks, before):
        total = jnp.zeros((span, model_width), jnp.float32)
        for shift in range(SF):
            picked = picks[shift]
            if shift < SF - 1:
                at_row = tail_rows - SF + 1 + shift
                picked = jnp.where(out_row == 0, before[at_row : at_row + 1], picked)
            total = total + jnp.dot(
                picked.astype(jnp.bfloat16), pool_held[shift], preferred_element_type=jnp.float32
            )
        own[half] = total
        sent[half] = total.astype(jnp.bfloat16)
        for step in range(1, head_count):
            swap_copy(half, step).start()

    def normed_half(half):
        total = own[half]
        for step in range(1, head_count):
            source = lax.rem(my_head + step, head_count)
            pltpu.make_async_remote_copy(
                src_ref=sent.at[half], dst_ref=taken.at[source, half],
                send_sem=swap_send.at[step, half], recv_sem=swap_recv.at[source, half],
                device_id={"head": source}, device_id_type=pl.DeviceIdType.MESH,
            ).wait_recv()
            total = total + taken[source, half].astype(jnp.float32)
        pooled = total.astype(jnp.bfloat16)
        pooled_all[half * span : (half + 1) * span, :] = pooled
        widened = pooled.astype(jnp.float32)
        squares = jnp.sum(widened * widened, axis=1, keepdims=True) / model_width
        return (widened * lax.rsqrt(squares + norm_epsilon) * gain[...]).astype(jnp.bfloat16)

    def project_half(half, normed):
        key_values[half * span : (half + 1) * span, :] = jnp.dot(
            normed, qkv_held[:, total_width:], preferred_element_type=jnp.float32
        ).astype(jnp.bfloat16)

    pair_base = span_order[me] * span
    own_tail = byte_rows[half_rows - tail_rows : half_rows, :].astype(jnp.float32)
    early_picks = pick_rows(0)
    pool_load.wait()
    tail_copies[1].wait_recv()
    pool(
        1, late_picks, jnp.where(pair_base == (count - 1) * span, own_tail, tails[1].astype(jnp.float32))
    )
    tail_copies[0].wait_recv()
    pool(0, early_picks, jnp.where(pair_base == 0, 0.0, tails[0].astype(jnp.float32)))
    qkv_load.wait()
    late_normed = normed_half(1)
    gathered[me] = jnp.dot(
        late_normed, qkv_held[:, :total_width], preferred_element_type=jnp.float32
    ).astype(jnp.bfloat16)

    pushes = []

    def push(slot, target):
        copy = pltpu.make_async_remote_copy(
            src_ref=gathered.at[slot], dst_ref=gathered.at[slot],
            send_sem=gather_send.at[len(pushes)], recv_sem=gather_recv.at[slot],
            device_id={"seq": target}, device_id_type=pl.DeviceIdType.MESH,
        )
        copy.start()
        pushes.append(copy)

    def landed(slot):
        pltpu.make_async_remote_copy(
            src_ref=gathered.at[slot], dst_ref=gathered.at[slot],
            send_sem=gather_send.at[0], recv_sem=gather_recv.at[slot],
            device_id={"seq": at(outer, middle, 1 - core)},
            device_id_type=pl.DeviceIdType.MESH,
        ).wait_recv()

    across = at(outer, 1 - middle, core)
    sibling = at(outer, middle, 1 - core)
    for step in range(1, outers):
        push(me, at(outer + step, middle, core))
    push(me, across)
    push(me, sibling)
    project_half(1, late_normed)
    for step in range(1, outers):
        slot = at(outer + step, middle, core)
        landed(slot)
        push(slot, across)
        push(slot, sibling)
    project_half(0, normed_half(0))
    shortened[...] = pooled_all[
        :, pl.ds(pl.multiple_of(my_head * features, LANES), features)
    ]
    for step in range(outers):
        slot = at(outer + step, 1 - middle, core)
        landed(slot)
        push(slot, sibling)
    for step in range(outers):
        landed(at(outer + step, middle, 1 - core))
        landed(at(outer + step, 1 - middle, 1 - core))

    blocks = count // 2
    chip = me // 2
    window_start = query_start[0]
    from_half = window_start - count * span
    first_place = lax.div(from_half, span)
    offset = from_half - first_place * span
    slot_base = 2 * count - 1 - first_place - span_order[0]
    first_base = pair_base
    second_base = (2 * count - 1) * span - pair_base
    pick_row = lax.broadcasted_iota(jnp.int32, (span, 2 * span), 0)
    pick_col = lax.broadcasted_iota(jnp.int32, (span, 2 * span), 1)
    pick = jnp.where(pick_col == pick_row + offset, 1.0, 0.0).astype(jnp.bfloat16)
    key_col = lax.broadcasted_iota(jnp.int32, (span, rows), 1)
    key_pos = jnp.where(key_col < span, first_base + key_col, second_base + key_col - span)
    ahead = key_pos - lax.broadcasted_iota(jnp.int32, (span, rows), 0) - window_start
    lane = lax.broadcasted_iota(jnp.int32, (span, LANES), 1)
    scale = width ** (-0.5)

    half_lane = lax.broadcasted_iota(jnp.int32, (span // 2, LANES), 1)

    def block_at(step):
        return lax.rem(chip + 1 + step, blocks)

    def give_copy(block):
        return pltpu.make_async_remote_copy(
            src_ref=parts.at[2 * block + 1 - core], dst_ref=given.at[block],
            send_sem=give_send.at[block], recv_sem=give_recv.at[block],
            device_id={"seq": sibling}, device_id_type=pl.DeviceIdType.MESH,
        )

    def part_copy(block, source):
        return pltpu.make_async_remote_copy(
            src_ref=merged.at[block], dst_ref=arrived.at[source],
            send_sem=part_send.at[block], recv_sem=part_recv.at[source],
            device_id={"seq": 2 * block + core}, device_id_type=pl.DeviceIdType.MESH,
        )

    def merge(block, into, place):
        give_copy(block).wait_recv()
        mine = 2 * block + core
        my_highs, my_totals = unpack_stats(parts[mine, :, total_width:].astype(jnp.float32))
        highs, totals = unpack_stats(given[block, :, total_width:].astype(jnp.float32))
        best = jnp.maximum(my_highs, highs)
        my_factor = jnp.exp(my_highs - best)
        factor = jnp.exp(highs - best)
        total = my_totals * my_factor + totals * factor
        for head in range(heads):
            columns = slice(head * width, (head + 1) * width)
            into[place, :, columns] = (
                parts[mine, :, columns].astype(jnp.float32) * my_factor[:, head : head + 1]
                + given[block, :, columns].astype(jnp.float32) * factor[:, head : head + 1]
            ).astype(jnp.bfloat16)
        used = half_lane < heads
        into[place, :, total_width:] = pack_stats(
            jnp.where(used, best, 0.0), jnp.where(used, total, 0.0)
        ).astype(jnp.bfloat16)

    def attend(step, carry):
        block = block_at(step)
        both = jnp.concatenate(
            [
                gathered[lax.rem(slot_base - block, count)],
                gathered[lax.rem(slot_base - block - 1, count)],
            ], axis=0
        )
        queries = jnp.dot(pick, both, preferred_element_type=jnp.float32).astype(jnp.bfloat16)
        allowed = ahead <= block * span
        highs = jnp.zeros((span, LANES), jnp.float32)
        totals = jnp.zeros((span, LANES), jnp.float32)
        for head in range(heads):
            base = head * width
            keys = key_values[:, base : base + width]
            values = key_values[:, total_width + base : total_width + base + width]
            scores = lax.dot_general(
                queries[:, head * width : (head + 1) * width], keys,
                (((1,), (1,)), ((), ())), preferred_element_type=jnp.float32,
            ) * scale
            scores = jnp.where(allowed, scores, masked_score)
            high = jnp.max(scores, axis=1, keepdims=True)
            weights = jnp.exp(scores - high).astype(jnp.bfloat16)
            total = jnp.sum(weights.astype(jnp.float32), axis=1, keepdims=True)
            summed = jnp.dot(weights, values, preferred_element_type=jnp.float32)
            summed = summed.astype(jnp.bfloat16)
            columns = slice(head * width, (head + 1) * width)
            parts[2 * block, :, columns] = summed[: span // 2]
            parts[2 * block + 1, :, columns] = summed[span // 2 :]
            highs = jnp.where(lane == head, high, highs)
            totals = jnp.where(lane == head, total, totals)
        packed = pack_stats(highs, totals).astype(jnp.bfloat16)
        parts[2 * block, :, total_width:] = packed[: span // 2]
        parts[2 * block + 1, :, total_width:] = packed[span // 2 :]
        give_copy(block).start()

        @pl.when(step > 0)
        def _():
            before = block_at(step - 1)
            merge(before, merged, before)
            part_copy(before, chip).start()

        return carry

    lax.fori_loop(0, blocks, attend, 0)
    merge(chip, arrived, chip)

    def settle(step, carry):
        other = lax.rem(chip + step, blocks)
        part_copy(other, chip).wait_send()
        part_copy(other, other).wait_recv()
        return carry

    lax.fori_loop(1, blocks, settle, 0)

    def given_away(block, carry):
        give_copy(block).wait_send()
        return carry

    lax.fori_loop(0, blocks, given_away, 0)
    for copy in pushes:
        copy.wait_send()
    for copy in tail_copies:
        copy.wait_send()
    for half in range(2):
        for step in range(1, head_count):
            swap_copy(half, step).wait_send()

    def stats_of(source):
        return unpack_stats(arrived[source, :, total_width:].astype(jnp.float32))

    top = lax.fori_loop(
        1, blocks, lambda source, best: jnp.maximum(best, stats_of(source)[0]), stats_of(0)[0]
    )
    def add(source, carry):
        denominator, pieces = carry
        highs, totals = stats_of(source)
        factor = jnp.exp(highs - top)
        pieces = tuple(
            pieces[head]
            + arrived[source, :, head * width : (head + 1) * width].astype(jnp.float32)
            * factor[:, head : head + 1]
            for head in range(heads)
        )
        return denominator + factor * totals, pieces

    empty = jnp.zeros((span // 2, width), jnp.float32)
    denominator, pieces = lax.fori_loop(
        0, blocks, add, (jnp.zeros((span // 2, LANES), jnp.float32), (empty,) * heads)
    )
    for head in range(heads):
        context[:, head * width : (head + 1) * width] = (
            pieces[head] / denominator[:, head : head + 1]
        ).astype(jnp.bfloat16)
    turned = jnp.concatenate([top, top], axis=0).T
    top_out[...] = turned[:heads, : span // 2] * width**0.5


def whole_kernel(
    span_order, query_start, byte_rows, gain, pool_weight, qkv_weight, count, head_count, heads, width
):
    span = byte_rows.shape[0] // (2 * SF)
    features = byte_rows.shape[1]
    model_width = pool_weight.shape[2]
    total_width = heads * width
    vmem = pl.BlockSpec(memory_space=pltpu.VMEM)
    return pl.pallas_call(
        functools.partial(attend_kernel, count, head_count, heads, width),
        out_shape=(
            jax.ShapeDtypeStruct((2 * span, features), jnp.bfloat16),
            jax.ShapeDtypeStruct((span // 2, total_width), jnp.bfloat16),
            jax.ShapeDtypeStruct((heads, span // 2), jnp.float32),
        ),
        in_specs=[
            pl.BlockSpec(memory_space=pltpu.SMEM),
            pl.BlockSpec(memory_space=pltpu.SMEM),
            pl.BlockSpec(memory_space=pl.ANY),
            vmem,
            pl.BlockSpec(memory_space=pl.ANY),
            pl.BlockSpec(memory_space=pl.ANY),
        ],
        out_specs=(vmem, vmem, vmem),
        scratch_shapes=[
            pltpu.VMEM(byte_rows.shape, jnp.bfloat16),
            pltpu.VMEM((2, 16, features), jnp.bfloat16),
            pltpu.VMEM(pool_weight.shape, jnp.bfloat16),
            pltpu.VMEM(qkv_weight.shape, jnp.bfloat16),
            pltpu.VMEM((2, span, model_width), jnp.float32),
            pltpu.VMEM((2, span, model_width), jnp.bfloat16),
            pltpu.VMEM((head_count, 2, span, model_width), jnp.bfloat16),
            pltpu.VMEM((2 * span, model_width), jnp.bfloat16),
            pltpu.VMEM((2 * span, 2 * total_width), jnp.bfloat16),
            pltpu.VMEM((count, span, total_width), jnp.bfloat16),
            pltpu.VMEM((count, span // 2, total_width + LANES), jnp.bfloat16),
            pltpu.VMEM((count // 2, span // 2, total_width + LANES), jnp.bfloat16),
            pltpu.VMEM((count // 2, span // 2, total_width + LANES), jnp.bfloat16),
            pltpu.VMEM((count // 2, span // 2, total_width + LANES), jnp.bfloat16),
            pltpu.SemaphoreType.DMA((3,)),
            pltpu.SemaphoreType.DMA((2,)),
            pltpu.SemaphoreType.DMA((2,)),
            pltpu.SemaphoreType.DMA((head_count, 2)),
            pltpu.SemaphoreType.DMA((head_count, 2)),
            pltpu.SemaphoreType.DMA((count,)),
            pltpu.SemaphoreType.DMA((count,)),
            pltpu.SemaphoreType.DMA((count // 2,)),
            pltpu.SemaphoreType.DMA((count // 2,)),
            pltpu.SemaphoreType.DMA((count // 2,)),
            pltpu.SemaphoreType.DMA((count // 2,)),
        ],
        compiler_params=pltpu.CompilerParams(
            collective_id=0, has_side_effects=True, vmem_limit_bytes=48 * 1024 * 1024
        ),
    )(span_order, query_start, byte_rows, gain, pool_weight, qkv_weight)


def body(byte_rows, pool_weight, norm_gain, qkv_weight, span_order, query_start):
    model_width, heads_here, _, head_width = qkv_weight.shape
    qkv_flat = qkv_weight.transpose(0, 2, 1, 3).reshape(model_width, -1)
    return whole_kernel(
        span_order, query_start, byte_rows, norm_gain.reshape(1, -1), pool_weight, qkv_flat,
        lax.axis_size("seq"), lax.axis_size("head"), heads_here, head_width,
    )


def solution(mesh):
    placed = (P("seq", "head"), P(None, "head", None), P(), P(None, "head", None, None), P(), P())
    return jax.shard_map(
        body,
        mesh=mesh,
        in_specs=placed,
        out_specs=(P("seq", "head"), P("seq", "head"), P("head", "seq")),
        check_vma=False,
    )
```

```python
import functools

import jax
import jax.numpy as jnp
from jax import lax
from jax.experimental import pallas as pl
from jax.experimental.pallas import tpu as pltpu
from jax.sharding import PartitionSpec as P

SF = 4


norm_epsilon = 1e-06
masked_score = -1e30


LANES = 128
STAT_STEP = 16


def pack_stats(highest, totals):
    high_top = highest.astype(jnp.bfloat16).astype(jnp.float32)
    rest = highest - high_top
    high_mid = rest.astype(jnp.bfloat16).astype(jnp.float32)
    high_low = rest - high_mid
    total_top = totals.astype(jnp.bfloat16).astype(jnp.float32)
    total_low = totals - total_top
    packed = high_top
    for place, piece in enumerate((high_mid, high_low, total_top, total_low)):
        packed = packed + pltpu.roll(piece, STAT_STEP * (place + 1), 1)
    return packed


def unpack_stats(packed):
    def piece(place):
        return pltpu.roll(packed, LANES - STAT_STEP * place, 1)

    return packed + piece(1) + piece(2), piece(3) + piece(4)


def attend_kernel(
    count, head_count, heads, width, span_order, query_start, rows_in, gain, pool_weight, qkv_weight,
    shortened, context, top_out,
    byte_rows, tails, pool_held, qkv_held, own, sent, taken, pooled_all, key_values,
    gathered, parts, given, merged, arrived,
    load_sem, tail_send, tail_recv, swap_send, swap_recv,
    gather_send, gather_recv, give_send, give_recv, part_send, part_recv,
):
    me = lax.axis_index("seq")
    my_head = lax.axis_index("head")
    core = lax.rem(me, 2)
    middle = lax.rem(me // 2, 2)
    outer = me // 4
    outers = count // 4
    rows = key_values.shape[0]
    span = rows // 2
    total_width = heads * width
    features = byte_rows.shape[1]
    model_width = pool_held.shape[2]
    half_rows = SF * span
    tail_rows = tails.shape[1]
    pool_load = pltpu.make_async_copy(pool_weight, pool_held, load_sem.at[0])
    qkv_load = pltpu.make_async_copy(qkv_weight, qkv_held, load_sem.at[1])
    rows_load = pltpu.make_async_copy(rows_in, byte_rows, load_sem.at[2])
    rows_load.start()
    pool_load.start()
    qkv_load.start()

    def at(outer_at, middle_at, core_at):
        return (lax.rem(outer_at, outers) * 2 + middle_at) * 2 + core_at

    barrier = pltpu.get_barrier_semaphore()

    def greet(step, carry):
        pl.semaphore_signal(
            barrier, inc=1, device_id={"seq": lax.rem(me + step, count)},
            device_id_type=pl.DeviceIdType.MESH,
        )
        return carry

    lax.fori_loop(1, count, greet, 0)
    def greet_head(step, carry):
        pl.semaphore_signal(
            barrier, inc=1, device_id={"head": lax.rem(my_head + step, head_count)},
            device_id_type=pl.DeviceIdType.MESH,
        )
        return carry

    lax.fori_loop(1, head_count, greet_head, 0)
    pool_row = lax.broadcasted_iota(jnp.int32, (span, half_rows), 0)
    pool_col = lax.broadcasted_iota(jnp.int32, (span, half_rows), 1)
    out_row = lax.broadcasted_iota(jnp.int32, (span, features), 0)

    def pick_rows(half):
        block = byte_rows[half * half_rows : (half + 1) * half_rows, :]
        picks = []
        for shift in range(SF):
            chosen = pool_col == SF * pool_row + (shift - SF + 1)
            chosen = jnp.where(chosen, 1.0, 0.0).astype(jnp.bfloat16)
            picks.append(jnp.dot(chosen, block, preferred_element_type=jnp.float32))
        return picks

    rows_load.wait()
    late_picks = pick_rows(1)
    pl.semaphore_wait(barrier, count - 1 + head_count - 1)

    def tail_copy(place, target):
        end = half_rows * (place + 1)
        return pltpu.make_async_remote_copy(
            src_ref=byte_rows.at[end - tail_rows : end], dst_ref=tails.at[place],
            send_sem=tail_send.at[place], recv_sem=tail_recv.at[place],
            device_id={"seq": target}, device_id_type=pl.DeviceIdType.MESH,
        )

    tail_copies = [
        tail_copy(0, lax.rem(me + 1, count)), tail_copy(1, lax.rem(me + count - 1, count))
    ]
    tail_copies[1].start()
    tail_copies[0].start()
    def swap_copy(half, step):
        target = lax.rem(my_head + step, head_count)
        return pltpu.make_async_remote_copy(
            src_ref=sent.at[half], dst_ref=taken.at[my_head, half],
            send_sem=swap_send.at[step, half], recv_sem=swap_recv.at[my_head, half],
            device_id={"head": target}, device_id_type=pl.DeviceIdType.MESH,
        )

    def pool(half, picks, before):
        total = jnp.zeros((span, model_width), jnp.float32)
        for shift in range(SF):
            picked = picks[shift]
            if shift < SF - 1:
                at_row = tail_rows - SF + 1 + shift
                picked = jnp.where(out_row == 0, before[at_row : at_row + 1], picked)
            total = total + jnp.dot(
                picked.astype(jnp.bfloat16), pool_held[shift], preferred_element_type=jnp.float32
            )
        own[half] = total
        sent[half] = total.astype(jnp.bfloat16)
        for step in range(1, head_count):
            swap_copy(half, step).start()

    def normed_half(half):
        total = own[half]
        for step in range(1, head_count):
            source = lax.rem(my_head + step, head_count)
            pltpu.make_async_remote_copy(
                src_ref=sent.at[half], dst_ref=taken.at[source, half],
                send_sem=swap_send.at[step, half], recv_sem=swap_recv.at[source, half],
                device_id={"head": source}, device_id_type=pl.DeviceIdType.MESH,
            ).wait_recv()
            total = total + taken[source, half].astype(jnp.float32)
        pooled = total.astype(jnp.bfloat16)
        pooled_all[half * span : (half + 1) * span, :] = pooled
        widened = pooled.astype(jnp.float32)
        squares = jnp.sum(widened * widened, axis=1, keepdims=True) / model_width
        return (widened * lax.rsqrt(squares + norm_epsilon) * gain[...]).astype(jnp.bfloat16)

    def project_half(half, normed):
        key_values[half * span : (half + 1) * span, :] = jnp.dot(
            normed, qkv_held[:, total_width:], preferred_element_type=jnp.float32
        ).astype(jnp.bfloat16)

    pair_base = span_order[me] * span
    own_tail = byte_rows[half_rows - tail_rows : half_rows, :].astype(jnp.float32)
    early_picks = pick_rows(0)
    pool_load.wait()
    tail_copies[1].wait_recv()
    pool(
        1, late_picks, jnp.where(pair_base == (count - 1) * span, own_tail, tails[1].astype(jnp.float32))
    )
    tail_copies[0].wait_recv()
    pool(0, early_picks, jnp.where(pair_base == 0, 0.0, tails[0].astype(jnp.float32)))
    qkv_load.wait()
    late_normed = normed_half(1)
    gathered[me] = jnp.dot(
        late_normed, qkv_held[:, :total_width], preferred_element_type=jnp.float32
    ).astype(jnp.bfloat16)

    across = at(outer, 1 - middle, core)
    sibling = at(outer, middle, 1 - core)
    above = at(outer + 1, middle, core)
    below = at(outer + outers - 1, middle, core)

    def push(slot, kind, target):
        return pltpu.make_async_remote_copy(
            src_ref=gathered.at[slot], dst_ref=gathered.at[slot],
            send_sem=gather_send.at[slot, kind], recv_sem=gather_recv.at[slot],
            device_id={"seq": target}, device_id_type=pl.DeviceIdType.MESH,
        )

    def spread(slot, up, down, do):
        if up:

            @pl.when(outer + 1 < outers)
            def _():
                do(push(slot, 0, above))

        if down:

            @pl.when(outer > 0)
            def _():
                do(push(slot, 1, below))

        do(push(slot, 2, across))
        do(push(slot, 3, sibling))

    def by_distance(middle_at, do):
        for step in range(1, outers):

            @pl.when(outer >= step)
            def _():
                do(at(outer + outers - step, middle_at, core), True)

            @pl.when(outer + step < outers)
            def _():
                do(at(outer + step, middle_at, core), False)

    def landed(slot):
        pltpu.make_async_remote_copy(
            src_ref=gathered.at[slot], dst_ref=gathered.at[slot],
            send_sem=gather_send.at[slot, 3], recv_sem=gather_recv.at[slot],
            device_id={"seq": at(outer, middle, 1 - core)},
            device_id_type=pl.DeviceIdType.MESH,
        ).wait_recv()

    def begin(copy):
        copy.start()

    def finish(copy):
        copy.wait_send()

    def pass_along(slot, from_below):
        landed(slot)
        spread(slot, from_below, not from_below, begin)

    def pass_over(slot, from_below):
        landed(slot)
        push(slot, 3, sibling).start()

    spread(me, True, True, begin)
    project_half(1, late_normed)
    by_distance(middle, pass_along)
    project_half(0, normed_half(0))
    shortened[...] = pooled_all[
        :, pl.ds(pl.multiple_of(my_head * features, LANES), features)
    ]
    pass_over(across, True)
    by_distance(1 - middle, pass_over)
    for step in range(outers):
        landed(at(outer + step, middle, 1 - core))
        landed(at(outer + step, 1 - middle, 1 - core))

    blocks = count // 2
    chip = me // 2
    window_start = query_start[0]
    from_half = window_start - count * span
    first_place = lax.div(from_half, span)
    offset = from_half - first_place * span
    slot_base = 2 * count - 1 - first_place - span_order[0]
    first_base = pair_base
    second_base = (2 * count - 1) * span - pair_base
    pick_row = lax.broadcasted_iota(jnp.int32, (span, 2 * span), 0)
    pick_col = lax.broadcasted_iota(jnp.int32, (span, 2 * span), 1)
    pick = jnp.where(pick_col == pick_row + offset, 1.0, 0.0).astype(jnp.bfloat16)
    key_col = lax.broadcasted_iota(jnp.int32, (span, rows), 1)
    key_pos = jnp.where(key_col < span, first_base + key_col, second_base + key_col - span)
    ahead = key_pos - lax.broadcasted_iota(jnp.int32, (span, rows), 0) - window_start
    lane = lax.broadcasted_iota(jnp.int32, (span, LANES), 1)
    scale = width ** (-0.5)

    half_lane = lax.broadcasted_iota(jnp.int32, (span // 2, LANES), 1)

    def block_at(step):
        return lax.rem(chip + 1 + step, blocks)

    def give_copy(block):
        return pltpu.make_async_remote_copy(
            src_ref=parts.at[2 * block + 1 - core], dst_ref=given.at[block],
            send_sem=give_send.at[block], recv_sem=give_recv.at[block],
            device_id={"seq": sibling}, device_id_type=pl.DeviceIdType.MESH,
        )

    def part_copy(block, source):
        return pltpu.make_async_remote_copy(
            src_ref=merged.at[block], dst_ref=arrived.at[source],
            send_sem=part_send.at[block], recv_sem=part_recv.at[source],
            device_id={"seq": 2 * block + core}, device_id_type=pl.DeviceIdType.MESH,
        )

    def merge(block, into, place):
        give_copy(block).wait_recv()
        mine = 2 * block + core
        my_highs, my_totals = unpack_stats(parts[mine, :, total_width:].astype(jnp.float32))
        highs, totals = unpack_stats(given[block, :, total_width:].astype(jnp.float32))
        best = jnp.maximum(my_highs, highs)
        my_factor = jnp.exp(my_highs - best)
        factor = jnp.exp(highs - best)
        total = my_totals * my_factor + totals * factor
        for head in range(heads):
            columns = slice(head * width, (head + 1) * width)
            into[place, :, columns] = (
                parts[mine, :, columns].astype(jnp.float32) * my_factor[:, head : head + 1]
                + given[block, :, columns].astype(jnp.float32) * factor[:, head : head + 1]
            ).astype(jnp.bfloat16)
        used = half_lane < heads
        into[place, :, total_width:] = pack_stats(
            jnp.where(used, best, 0.0), jnp.where(used, total, 0.0)
        ).astype(jnp.bfloat16)

    def attend(step, carry):
        block = block_at(step)
        both = jnp.concatenate(
            [
                gathered[lax.rem(slot_base - block, count)],
                gathered[lax.rem(slot_base - block - 1, count)],
            ], axis=0
        )
        queries = jnp.dot(pick, both, preferred_element_type=jnp.float32).astype(jnp.bfloat16)
        allowed = ahead <= block * span
        highs = jnp.zeros((span, LANES), jnp.float32)
        totals = jnp.zeros((span, LANES), jnp.float32)
        for head in range(heads):
            base = head * width
            keys = key_values[:, base : base + width]
            values = key_values[:, total_width + base : total_width + base + width]
            scores = lax.dot_general(
                queries[:, head * width : (head + 1) * width], keys,
                (((1,), (1,)), ((), ())), preferred_element_type=jnp.float32,
            ) * scale
            scores = jnp.where(allowed, scores, masked_score)
            high = jnp.max(scores, axis=1, keepdims=True)
            weights = jnp.exp(scores - high).astype(jnp.bfloat16)
            total = jnp.sum(weights.astype(jnp.float32), axis=1, keepdims=True)
            summed = jnp.dot(weights, values, preferred_element_type=jnp.float32)
            summed = summed.astype(jnp.bfloat16)
            columns = slice(head * width, (head + 1) * width)
            parts[2 * block, :, columns] = summed[: span // 2]
            parts[2 * block + 1, :, columns] = summed[span // 2 :]
            highs = jnp.where(lane == head, high, highs)
            totals = jnp.where(lane == head, total, totals)
        packed = pack_stats(highs, totals).astype(jnp.bfloat16)
        parts[2 * block, :, total_width:] = packed[: span // 2]
        parts[2 * block + 1, :, total_width:] = packed[span // 2 :]
        give_copy(block).start()

        @pl.when(step > 0)
        def _():
            before = block_at(step - 1)
            merge(before, merged, before)
            part_copy(before, chip).start()

        return carry

    lax.fori_loop(0, blocks, attend, 0)
    merge(chip, arrived, chip)

    def settle(step, carry):
        other = lax.rem(chip + step, blocks)
        part_copy(other, chip).wait_send()
        part_copy(other, other).wait_recv()
        return carry

    lax.fori_loop(1, blocks, settle, 0)

    def given_away(block, carry):
        give_copy(block).wait_send()
        return carry

    lax.fori_loop(0, blocks, given_away, 0)
    spread(me, True, True, finish)
    by_distance(middle, lambda slot, from_below: spread(slot, from_below, not from_below, finish))
    push(across, 3, sibling).wait_send()
    by_distance(1 - middle, lambda slot, from_below: push(slot, 3, sibling).wait_send())
    for copy in tail_copies:
        copy.wait_send()
    for half in range(2):
        for step in range(1, head_count):
            swap_copy(half, step).wait_send()

    def stats_of(source):
        return unpack_stats(arrived[source, :, total_width:].astype(jnp.float32))

    top = lax.fori_loop(
        1, blocks, lambda source, best: jnp.maximum(best, stats_of(source)[0]), stats_of(0)[0]
    )
    def add(source, carry):
        denominator, pieces = carry
        highs, totals = stats_of(source)
        factor = jnp.exp(highs - top)
        pieces = tuple(
            pieces[head]
            + arrived[source, :, head * width : (head + 1) * width].astype(jnp.float32)
            * factor[:, head : head + 1]
            for head in range(heads)
        )
        return denominator + factor * totals, pieces

    empty = jnp.zeros((span // 2, width), jnp.float32)
    denominator, pieces = lax.fori_loop(
        0, blocks, add, (jnp.zeros((span // 2, LANES), jnp.float32), (empty,) * heads)
    )
    for head in range(heads):
        context[:, head * width : (head + 1) * width] = (
            pieces[head] / denominator[:, head : head + 1]
        ).astype(jnp.bfloat16)
    turned = jnp.concatenate([top, top], axis=0).T
    top_out[...] = turned[:heads, : span // 2] * width**0.5


def whole_kernel(
    span_order, query_start, byte_rows, gain, pool_weight, qkv_weight, count, head_count, heads, width
):
    span = byte_rows.shape[0] // (2 * SF)
    features = byte_rows.shape[1]
    model_width = pool_weight.shape[2]
    total_width = heads * width
    vmem = pl.BlockSpec(memory_space=pltpu.VMEM)
    return pl.pallas_call(
        functools.partial(attend_kernel, count, head_count, heads, width),
        out_shape=(
            jax.ShapeDtypeStruct((2 * span, features), jnp.bfloat16),
            jax.ShapeDtypeStruct((span // 2, total_width), jnp.bfloat16),
            jax.ShapeDtypeStruct((heads, span // 2), jnp.float32),
        ),
        in_specs=[
            pl.BlockSpec(memory_space=pltpu.SMEM),
            pl.BlockSpec(memory_space=pltpu.SMEM),
            pl.BlockSpec(memory_space=pl.ANY),
            vmem,
            pl.BlockSpec(memory_space=pl.ANY),
            pl.BlockSpec(memory_space=pl.ANY),
        ],
        out_specs=(vmem, vmem, vmem),
        scratch_shapes=[
            pltpu.VMEM(byte_rows.shape, jnp.bfloat16),
            pltpu.VMEM((2, 16, features), jnp.bfloat16),
            pltpu.VMEM(pool_weight.shape, jnp.bfloat16),
            pltpu.VMEM(qkv_weight.shape, jnp.bfloat16),
            pltpu.VMEM((2, span, model_width), jnp.float32),
            pltpu.VMEM((2, span, model_width), jnp.bfloat16),
            pltpu.VMEM((head_count, 2, span, model_width), jnp.bfloat16),
            pltpu.VMEM((2 * span, model_width), jnp.bfloat16),
            pltpu.VMEM((2 * span, 2 * total_width), jnp.bfloat16),
            pltpu.VMEM((count, span, total_width), jnp.bfloat16),
            pltpu.VMEM((count, span // 2, total_width + LANES), jnp.bfloat16),
            pltpu.VMEM((count // 2, span // 2, total_width + LANES), jnp.bfloat16),
            pltpu.VMEM((count // 2, span // 2, total_width + LANES), jnp.bfloat16),
            pltpu.VMEM((count // 2, span // 2, total_width + LANES), jnp.bfloat16),
            pltpu.SemaphoreType.DMA((3,)),
            pltpu.SemaphoreType.DMA((2,)),
            pltpu.SemaphoreType.DMA((2,)),
            pltpu.SemaphoreType.DMA((head_count, 2)),
            pltpu.SemaphoreType.DMA((head_count, 2)),
            pltpu.SemaphoreType.DMA((count, 4)),
            pltpu.SemaphoreType.DMA((count,)),
            pltpu.SemaphoreType.DMA((count // 2,)),
            pltpu.SemaphoreType.DMA((count // 2,)),
            pltpu.SemaphoreType.DMA((count // 2,)),
            pltpu.SemaphoreType.DMA((count // 2,)),
        ],
        compiler_params=pltpu.CompilerParams(
            collective_id=0, has_side_effects=True, vmem_limit_bytes=48 * 1024 * 1024
        ),
    )(span_order, query_start, byte_rows, gain, pool_weight, qkv_weight)


def body(byte_rows, pool_weight, norm_gain, qkv_weight, span_order, query_start):
    model_width, heads_here, _, head_width = qkv_weight.shape
    qkv_flat = qkv_weight.transpose(0, 2, 1, 3).reshape(model_width, -1)
    return whole_kernel(
        span_order, query_start, byte_rows, norm_gain.reshape(1, -1), pool_weight, qkv_flat,
        lax.axis_size("seq"), lax.axis_size("head"), heads_here, head_width,
    )


def solution(mesh):
    placed = (P("seq", "head"), P(None, "head", None), P(), P(None, "head", None, None), P(), P())
    return jax.shard_map(
        body,
        mesh=mesh,
        in_specs=placed,
        out_specs=(P("seq", "head"), P("seq", "head"), P("head", "seq")),
        check_vma=False,
    )
```
